32 devices in a mesh: groups: 2 (over y), row: 4 (over z), col: 2 (over x), rep: 2 (over core).
Axes of the slice: x: 2, y: 2, z: 4, core: 2. Of those that a mesh axis runs over, the one named last changes fastest.
Arguments:
- kernel: float32 [32768, 16384], P(('groups', 'row'), ('col', 'rep')), parts along dimension 0, may hold values from 0 to 2, as said below
- source: float32 [64, 16384], P('groups', 'row'), parts along dimension 0, may hold values from 0.5 to 2, as said below
- target: float32 [64, 16384], P('groups', ('col', 'rep')), parts along dimension 0, may hold values from 0.5 to 2, as said below
Outputs:
- left_scale: float32 [64, 16384], P('groups', 'row'), parts along dimension 0
- right_scale: float32 [64, 16384], P('groups', ('col', 'rep')), parts along dimension 0
- errors: float32 [6, 32], P('groups'), parts along dimension 0
The draws below stay inside these ranges and needn't reach their ends.
There are 2 independent parts, one for each index of `groups`. The reference program is written for one: setup_inputs(seed, part) draws one part's arguments, and reference() takes and returns one part's arrays. A program takes and returns all parts, laid end to end along the dimension named above; each array names one. Nothing has to cross between parts.
Inputs may be any that keep to these rules, and one draw needn't show every extreme that they name: `kernel`: every entry is positive. `source`: every entry is positive. `target`: every entry is positive.
All inputs are finite; a program needn't handle non-finite values.
Results may differ from the reference program's by a relative error of at most 0.0001.
Values sent between devices are 32-bit elements; how exact they have to be, the bound alone decides.
A program may use at most 128 MiB of HBM per device.

```python
import math
import jax
import jax.numpy as jnp
from jax import lax

N = 16384
PAIRS = 32
ITERS = 3


def support_points(key):
    folded = jax.random.fold_in(key, 31)
    point_key, sink_key = jax.random.split(folded)
    source_points = jax.random.uniform(point_key, (N, 3), jnp.float32)
    target_points = jax.random.uniform(sink_key, (N, 3), jnp.float32)
    return (source_points, target_points)


def draw_kernel(key, part):
    source_points, target_points = support_points(key)
    row_key, col_key = jax.random.split(jax.random.fold_in(key, 11))
    top = math.log(10.0)
    spread = 0.025
    rows_log = jax.random.uniform(row_key, (N, 1), jnp.float32, 0.0, top)
    cols_log = jax.random.uniform(col_key, (1, N), jnp.float32, 0.0, top)
    source_norms = jnp.sum(source_points * source_points, axis=1)
    target_norms = jnp.sum(target_points * target_points, axis=1)
    cross = jnp.dot(source_points, target_points.T, precision=lax.Precision.HIGHEST)
    squared = jnp.maximum(source_norms[:, None] + target_norms[None, :] - 2.0 * cross, 0.0)
    raw = jnp.exp(rows_log + cols_log) * (jnp.exp(-squared / spread) + 0.005)
    return raw * (N / jnp.sum(raw))


def marginal_draw(folded):
    values = jnp.exp(jax.random.uniform(folded, (PAIRS, N), jnp.float32, math.log(0.5), math.log(2.0)))
    return values


def draw_source(key, part):
    return marginal_draw(jax.random.fold_in(key, 41))


def draw_target(key, part):
    return marginal_draw(jax.random.fold_in(key, 23))


def setup_inputs(seed: int = 0, part: int = 0) -> dict:
    keys = jax.random.split(jax.random.key(seed), 4)
    part_keys = jax.random.split(jax.random.fold_in(keys[3], part), 4)
    return {
        "kernel": draw_kernel(jax.random.fold_in(jax.random.fold_in(keys[3], part), 71), part),
        "source": draw_source(jax.random.fold_in(jax.random.fold_in(keys[3], part), 71), part),
        "target": draw_target(jax.random.fold_in(jax.random.fold_in(keys[3], part), 71), part),
    }


def reference(kernel, source, target):
    right_scale = jnp.ones(target.shape, jnp.float32)
    errors = []
    left_scale = source
    for step in range(ITERS):
        kv = lax.dot_general(right_scale, kernel, (((1,), (1,)), ((), ())), precision=lax.Precision.HIGHEST)
        left_scale = source / kv
        ktu = jnp.dot(left_scale, kernel, precision=lax.Precision.HIGHEST)
        errors.append(jnp.sum(jnp.abs(right_scale * ktu - target), axis=1) / N)
        right_scale = target / ktu
    return left_scale, right_scale, jnp.stack(errors)
```

```python
import functools

import jax
import jax.numpy as jnp
from jax import lax
from jax.experimental import pallas as pl
from jax.experimental.pallas import tpu as pltpu
from jax.sharding import PartitionSpec as P

ITERS = 3
BLOCK = 256
CHUNK = 1024
LAG = 3
MESH = pl.DeviceIdType.MESH


def split(x):
    hi = x.astype(jnp.bfloat16)
    return hi, (x - hi.astype(jnp.float32)).astype(jnp.bfloat16)


def body(R, C, k_hbm, src, tgt, u_out, v_out, e_out,
         kf, kh, kl, vhl, acc, red, rsrx, vbuf, part, rx1, rx2, eb, erx1, erx2,
         ksem, s1, r1, s2, r2, srs, rrs, sag, rag, se, re):
    rows, cols = k_hbm.shape
    pairs = src.shape[0]
    nb = rows // BLOCK
    pr = pairs // R
    ring = kh.shape[0]
    me_r = lax.axis_index("row")
    me_c = lax.axis_index("col")
    me_k = lax.axis_index("rep")
    other = 1 - me_k

    def load(b):
        b = lax.rem(b, nb)
        return pltpu.make_async_copy(
            k_hbm.at[pl.ds(pl.multiple_of(b * BLOCK, BLOCK), BLOCK), :],
            kf.at[lax.rem(b, 2)], ksem.at[lax.rem(b, 2)])

    load(0).start()
    load(1).start()

    barrier = pltpu.get_barrier_semaphore()
    pl.semaphore_signal(barrier, inc=1, device_id={"rep": other}, device_id_type=MESH)
    for k in range(1, C):
        pl.semaphore_signal(barrier, inc=1, device_id={"col": lax.rem(me_c + k, C)}, device_id_type=MESH)
    for k in range(1, R):
        pl.semaphore_signal(barrier, inc=1, device_id={"row": lax.rem(me_r + k, R)}, device_id_type=MESH)
    pl.semaphore_wait(barrier, 1 + (C - 1) + (R - 1))

    vhl[0:pairs, :] = jnp.ones((pairs, cols), jnp.bfloat16)
    vhl[pairs:, :] = jnp.zeros((pairs, cols), jnp.bfloat16)
    vbuf[0, :, :, 0:cols] = jnp.ones((R, pr, cols), jnp.float32)

    def to_rep(src_ref, dst_ref, ssem, rsem):
        return pltpu.make_async_remote_copy(
            src_ref=src_ref, dst_ref=dst_ref, send_sem=ssem, recv_sem=rsem,
            device_id={"rep": other}, device_id_type=MESH)

    def to_col(k, src_ref, dst_ref, ssem, rsem):
        return pltpu.make_async_remote_copy(
            src_ref=src_ref, dst_ref=dst_ref, send_sem=ssem, recv_sem=rsem,
            device_id={"col": lax.rem(me_c + k, C)}, device_id_type=MESH)

    def to_row(k, src_ref, dst_ref, ssem, rsem):
        return pltpu.make_async_remote_copy(
            src_ref=src_ref, dst_ref=dst_ref, send_sem=ssem, recv_sem=rsem,
            device_id={"row": lax.rem(me_r + k, R)}, device_id_type=MESH)

    def first(g):
        return to_rep(part.at[g], rx1.at[g], s1.at[g], r1.at[g])

    for t in range(ITERS):
        base = (t % 2) * nb
        acc[...] = jnp.zeros_like(acc)

        @pl.loop(0, nb + LAG)
        def _(s):
            @pl.when(s < nb)
            def _():
                slot = lax.rem(s, 2)
                hold = lax.rem(s, ring)
                load(s).wait()
                total = jnp.zeros((2 * pairs, BLOCK), jnp.float32)
                for c in range(0, cols, CHUNK):
                    hi, lo = split(kf[slot, :, c:c + CHUNK])
                    kh[hold, :, c:c + CHUNK] = hi
                    kl[hold, :, c:c + CHUNK] = lo
                    v = vhl[:, c:c + CHUNK]
                    dims = (((1,), (1,)), ((), ()))
                    total += lax.dot_general(v, hi, dims, preferred_element_type=jnp.float32)
                    total += lax.dot_general(v, lo, dims, preferred_element_type=jnp.float32)
                part[base + s] = total[:pairs] + total[pairs:]
                first(base + s).start()
                if t < ITERS - 1:
                    load(s + 2).start()
                else:
                    @pl.when(s + 2 < nb)
                    def _():
                        load(s + 2).start()

            @pl.when((s >= 1) & (s <= nb))
            def _():
                g = base + s - 1
                first(g).wait()
                rx2[g, me_c] = part[g] + rx1[g]
                for k in range(1, C):
                    to_col(k, rx2.at[g, me_c], rx2.at[g, me_c], s2.at[g, k], r2.at[g, k]).start()

            @pl.when(s >= LAG)
            def _():
                b = s - LAG
                g = base + b
                hold = lax.rem(b, ring)
                for k in range(1, C):
                    peer = lax.rem(me_c + (C - k), C)
                    to_col(k, rx2.at[g, peer], rx2.at[g, peer], s2.at[g, k], r2.at[g, k]).wait()
                kv = rx2[g, 0]
                for c in range(1, C):
                    kv += rx2[g, c]
                at = pl.ds(pl.multiple_of(b * BLOCK, BLOCK), BLOCK)
                u = src[:, at] / kv
                u_out[:, at] = u
                hi, lo = split(u)
                uhl = jnp.concatenate([hi, lo], axis=0)
                acc[...] += (jnp.dot(uhl, kh[hold], preferred_element_type=jnp.float32)
                             + jnp.dot(uhl, kl[hold], preferred_element_type=jnp.float32))

        for q in range(R):
            red[q] = acc[q * pr:(q + 1) * pr, :] + acc[pairs + q * pr:pairs + (q + 1) * pr, :]
        for k in range(1, R):
            to_row(k, red.at[lax.rem(me_r + k, R)], rsrx.at[t, me_r], srs.at[k], rrs.at[k]).start()
        total = red[me_r]
        for k in range(1, R):
            peer = lax.rem(me_r + (R - k), R)
            to_row(k, red.at[lax.rem(me_r + k, R)], rsrx.at[t, peer], srs.at[k], rrs.at[k]).wait()
            total += rsrx[t, peer]
        goal = tgt[me_r]
        diff = jnp.abs(vbuf[t, me_r, :, 0:cols] * total - goal)
        lanes = diff[:, 0:128]
        for c in range(128, cols, 128):
            lanes += diff[:, c:c + 128]
        vbuf[t + 1, me_r, :, 0:cols] = goal / total
        vbuf[t + 1, me_r, :, cols:cols + 128] = lanes
        for k in range(1, R):
            to_row(k, vbuf.at[t + 1, me_r], vbuf.at[t + 1, me_r], sag.at[k], rag.at[k]).start()
        for k in range(1, R):
            peer = lax.rem(me_r + (R - k), R)
            to_row(k, vbuf.at[t + 1, peer], vbuf.at[t + 1, peer], sag.at[k], rag.at[k]).wait()
        full = jnp.concatenate([vbuf[t + 1, q, :, 0:cols] for q in range(R)], axis=0)
        if t < ITERS - 1:
            hi, lo = split(full)
            vhl[0:pairs, :] = hi
            vhl[pairs:, :] = lo
        else:
            v_out[...] = full
        eb[t] = jnp.concatenate([vbuf[t + 1, q, :, cols:cols + 128] for q in range(R)], axis=0)

    swap = to_rep(eb, erx1, se.at[0], re.at[0])
    swap.start()
    swap.wait()
    erx2[me_c] = eb[...] + erx1[...]
    for k in range(1, C):
        to_col(k, erx2.at[me_c], erx2.at[me_c], se.at[k], re.at[k]).start()
    for k in range(1, C):
        peer = lax.rem(me_c + (C - k), C)
        to_col(k, erx2.at[peer], erx2.at[peer], se.at[k], re.at[k]).wait()
    e = erx2[0]
    for c in range(1, C):
        e += erx2[c]
    e_out[...] = e


def local(R, C, D, kernel, source, target):
    rows, cols = kernel.shape
    pairs = source.shape[0]
    pr = pairs // R
    nb = rows // BLOCK
    f32, bf16 = jnp.float32, jnp.bfloat16
    dma = pltpu.SemaphoreType.DMA
    vmem = pl.BlockSpec(memory_space=pltpu.VMEM)
    ring = LAG + 1
    u, v, e = pl.pallas_call(
        functools.partial(body, R, C),
        out_shape=(
            jax.ShapeDtypeStruct((pairs, rows), f32),
            jax.ShapeDtypeStruct((pairs, cols), f32),
            jax.ShapeDtypeStruct((ITERS, pairs, 128), f32),
        ),
        in_specs=[pl.BlockSpec(memory_space=pl.ANY), vmem, vmem],
        out_specs=(vmem, vmem, vmem),
        scratch_shapes=[
            pltpu.VMEM((2, BLOCK, cols), f32),
            pltpu.VMEM((ring, BLOCK, cols), bf16),
            pltpu.VMEM((ring, BLOCK, cols), bf16),
            pltpu.VMEM((2 * pairs, cols), bf16),
            pltpu.VMEM((2 * pairs, cols), f32),
            pltpu.VMEM((R, pr, cols), f32),
            pltpu.VMEM((ITERS, R, pr, cols), f32),
            pltpu.VMEM((ITERS + 1, R, pr, cols + 128), f32),
            pltpu.VMEM((2 * nb, pairs, BLOCK), f32),
            pltpu.VMEM((2 * nb, pairs, BLOCK), f32),
            pltpu.VMEM((2 * nb, C, pairs, BLOCK), f32),
            pltpu.VMEM((ITERS, pairs, 128), f32),
            pltpu.VMEM((ITERS, pairs, 128), f32),
            pltpu.VMEM((C, ITERS, pairs, 128), f32),
            dma((2,)),
            dma((2 * nb,)), dma((2 * nb,)),
            dma((2 * nb, C)), dma((2 * nb, C)),
            dma((R,)), dma((R,)), dma((R,)), dma((R,)),
            dma((C,)), dma((C,)),
        ],
        compiler_params=pltpu.CompilerParams(
            collective_id=0, has_side_effects=True, vmem_limit_bytes=60 << 20),
    )(kernel, source, target.reshape(R, pr, cols))
    return u, v, jnp.sum(e, axis=2) / (cols * D)


def solution(mesh):
    R, C, K = (mesh.shape[a] for a in ("row", "col", "rep"))
    return jax.shard_map(
        functools.partial(local, R, C, C * K),
        mesh=mesh,
        in_specs=(
            P(("groups", "row"), ("col", "rep")),
            P("groups", "row"),
            P("groups", ("col", "rep")),
        ),
        out_specs=(P("groups", "row"), P("groups", ("col", "rep")), P("groups", None)),
        check_vma=False,
    )
```

```python
import functools

import jax
import jax.numpy as jnp
from jax import lax
from jax.experimental import pallas as pl
from jax.experimental.pallas import tpu as pltpu
from jax.sharding import PartitionSpec as P

ITERS = 3
BLOCK = 256
CHUNK = 1024
LAG = 3
KEPT = 6
MESH = pl.DeviceIdType.MESH


def split(x):
    hi = x.astype(jnp.bfloat16)
    return hi, (x - hi.astype(jnp.float32)).astype(jnp.bfloat16)


def body(R, C, k_hbm, src, tgt, u_out, v_out, e_out,
         kf, kh, kl, vhl, acc, red, rsrx, vbuf, part, rx1, rx2, eb, erx1, erx2,
         ksem, s1, r1, s2, r2, srs, rrs, sag, rag, se, re):
    rows, cols = k_hbm.shape
    pairs = src.shape[0]
    nb = rows // BLOCK
    pr = pairs // R
    kept = min(KEPT, nb - 2)
    ring = kh.shape[0] - kept

    def home(b):
        return jnp.where(b < kept, b, kept + lax.rem(b, ring))

    me_r = lax.axis_index("row")
    me_c = lax.axis_index("col")
    me_k = lax.axis_index("rep")
    other = 1 - me_k

    def load(b):
        return pltpu.make_async_copy(
            k_hbm.at[pl.ds(pl.multiple_of(b * BLOCK, BLOCK), BLOCK), :],
            kf.at[lax.rem(b, 2)], ksem.at[lax.rem(b, 2)])

    load(0).start()
    load(1).start()

    barrier = pltpu.get_barrier_semaphore()
    pl.semaphore_signal(barrier, inc=1, device_id={"rep": other}, device_id_type=MESH)
    for k in range(1, C):
        pl.semaphore_signal(barrier, inc=1, device_id={"col": lax.rem(me_c + k, C)}, device_id_type=MESH)
    for k in range(1, R):
        pl.semaphore_signal(barrier, inc=1, device_id={"row": lax.rem(me_r + k, R)}, device_id_type=MESH)
    pl.semaphore_wait(barrier, 1 + (C - 1) + (R - 1))

    vbuf[0, :, :, 0:cols] = jnp.ones((R, pr, cols), jnp.float32)

    def to_rep(src_ref, dst_ref, ssem, rsem):
        return pltpu.make_async_remote_copy(
            src_ref=src_ref, dst_ref=dst_ref, send_sem=ssem, recv_sem=rsem,
            device_id={"rep": other}, device_id_type=MESH)

    def to_col(k, src_ref, dst_ref, ssem, rsem):
        return pltpu.make_async_remote_copy(
            src_ref=src_ref, dst_ref=dst_ref, send_sem=ssem, recv_sem=rsem,
            device_id={"col": lax.rem(me_c + k, C)}, device_id_type=MESH)

    def to_row(k, src_ref, dst_ref, ssem, rsem):
        return pltpu.make_async_remote_copy(
            src_ref=src_ref, dst_ref=dst_ref, send_sem=ssem, recv_sem=rsem,
            device_id={"row": lax.rem(me_r + k, R)}, device_id_type=MESH)

    def first(g):
        return to_rep(part.at[g], rx1.at[g], s1.at[g], r1.at[g])

    for t in range(ITERS):
        base = (t % 2) * nb
        acc[...] = jnp.zeros_like(acc)

        @pl.loop(0, nb + LAG)
        def _(s):
            @pl.when(s < nb)
            def _():
                hold = home(s)
                fresh = (s >= kept) if t > 0 else (s >= 0)
                dims = (((1,), (1,)), ((), ()))

                @pl.when(fresh)
                def _():
                    slot = lax.rem(s, 2)
                    load(s).wait()
                    if t == 0:
                        lanes = jnp.zeros((BLOCK, 128), jnp.float32)
                        for c in range(0, cols, CHUNK):
                            x = kf[slot, :, c:c + CHUNK]
                            hi, lo = split(x)
                            kh[hold, :, c:c + CHUNK] = hi
                            kl[hold, :, c:c + CHUNK] = lo
                            for d in range(0, CHUNK, 128):
                                lanes += x[:, d:d + 128]
                        hi, lo = split(lanes)
                        one = jnp.ones((pairs, 128), jnp.bfloat16)
                        part[base + s] = (lax.dot_general(one, hi, dims, preferred_element_type=jnp.float32)
                                          + lax.dot_general(one, lo, dims, preferred_element_type=jnp.float32))
                    else:
                        total = jnp.zeros((2 * pairs, BLOCK), jnp.float32)
                        for c in range(0, cols, CHUNK):
                            hi, lo = split(kf[slot, :, c:c + CHUNK])
                            kh[hold, :, c:c + CHUNK] = hi
                            kl[hold, :, c:c + CHUNK] = lo
                            v = vhl[:, c:c + CHUNK]
                            total += lax.dot_general(v, hi, dims, preferred_element_type=jnp.float32)
                            total += lax.dot_general(v, lo, dims, preferred_element_type=jnp.float32)
                        part[base + s] = total[:pairs] + total[pairs:]

                    @pl.when(s + 2 < nb)
                    def _():
                        load(s + 2).start()
                    if t < ITERS - 1:
                        @pl.when(s + 2 >= nb)
                        def _():
                            load(s + 2 - nb + kept).start()

                if t > 0:
                    @pl.when(s < kept)
                    def _():
                        v = vhl[...]
                        total = (lax.dot_general(v, kh[hold], dims, preferred_element_type=jnp.float32)
                                 + lax.dot_general(v, kl[hold], dims, preferred_element_type=jnp.float32))
                        part[base + s] = total[:pairs] + total[pairs:]

                first(base + s).start()

            @pl.when((s >= 1) & (s <= nb))
            def _():
                g = base + s - 1
                first(g).wait()
                rx2[g, me_c] = part[g] + rx1[g]
                for k in range(1, C):
                    to_col(k, rx2.at[g, me_c], rx2.at[g, me_c], s2.at[g, k], r2.at[g, k]).start()

            @pl.when(s >= LAG)
            def _():
                b = s - LAG
                g = base + b
                hold = home(b)
                for k in range(1, C):
                    peer = lax.rem(me_c + (C - k), C)
                    to_col(k, rx2.at[g, peer], rx2.at[g, peer], s2.at[g, k], r2.at[g, k]).wait()
                kv = rx2[g, 0]
                for c in range(1, C):
                    kv += rx2[g, c]
                at = pl.ds(pl.multiple_of(b * BLOCK, BLOCK), BLOCK)
                u = src[:, at] / kv
                u_out[:, at] = u
                hi, lo = split(u)
                uhl = jnp.concatenate([hi, lo], axis=0)
                acc[...] += (jnp.dot(uhl, kh[hold], preferred_element_type=jnp.float32)
                             + jnp.dot(uhl, kl[hold], preferred_element_type=jnp.float32))

        for q in range(R):
            red[q] = acc[q * pr:(q + 1) * pr, :] + acc[pairs + q * pr:pairs + (q + 1) * pr, :]
        for k in range(1, R):
            to_row(k, red.at[lax.rem(me_r + k, R)], rsrx.at[me_r], srs.at[k], rrs.at[k]).start()
        total = red[me_r]
        for k in range(1, R):
            peer = lax.rem(me_r + (R - k), R)
            to_row(k, red.at[lax.rem(me_r + k, R)], rsrx.at[peer], srs.at[k], rrs.at[k]).wait()
            total += rsrx[peer]
        goal = tgt[me_r]
        diff = jnp.abs(vbuf[t, me_r, :, 0:cols] * total - goal)
        lanes = diff[:, 0:128]
        for c in range(128, cols, 128):
            lanes += diff[:, c:c + 128]
        vbuf[t + 1, me_r, :, 0:cols] = goal / total
        vbuf[t + 1, me_r, :, cols:cols + 128] = lanes
        for k in range(1, R):
            to_row(k, vbuf.at[t + 1, me_r], vbuf.at[t + 1, me_r], sag.at[k], rag.at[k]).start()
        for k in range(1, R):
            peer = lax.rem(me_r + (R - k), R)
            to_row(k, vbuf.at[t + 1, peer], vbuf.at[t + 1, peer], sag.at[k], rag.at[k]).wait()
        full = jnp.concatenate([vbuf[t + 1, q, :, 0:cols] for q in range(R)], axis=0)
        if t < ITERS - 1:
            hi, lo = split(full)
            vhl[0:pairs, :] = hi
            vhl[pairs:, :] = lo
        else:
            v_out[...] = full
        eb[t] = jnp.concatenate([vbuf[t + 1, q, :, cols:cols + 128] for q in range(R)], axis=0)

    swap = to_rep(eb, erx1, se.at[0], re.at[0])
    swap.start()
    swap.wait()
    erx2[me_c] = eb[...] + erx1[...]
    for k in range(1, C):
        to_col(k, erx2.at[me_c], erx2.at[me_c], se.at[k], re.at[k]).start()
    for k in range(1, C):
        peer = lax.rem(me_c + (C - k), C)
        to_col(k, erx2.at[peer], erx2.at[peer], se.at[k], re.at[k]).wait()
    e = erx2[0]
    for c in range(1, C):
        e += erx2[c]
    e_out[...] = e


def local(R, C, D, kernel, source, target):
    rows, cols = kernel.shape
    pairs = source.shape[0]
    pr = pairs // R
    nb = rows // BLOCK
    f32, bf16 = jnp.float32, jnp.bfloat16
    dma = pltpu.SemaphoreType.DMA
    vmem = pl.BlockSpec(memory_space=pltpu.VMEM)
    ring = LAG + 1 + min(KEPT, nb - 2)
    u, v, e = pl.pallas_call(
        functools.partial(body, R, C),
        out_shape=(
            jax.ShapeDtypeStruct((pairs, rows), f32),
            jax.ShapeDtypeStruct((pairs, cols), f32),
            jax.ShapeDtypeStruct((ITERS, pairs, 128), f32),
        ),
        in_specs=[pl.BlockSpec(memory_space=pl.ANY), vmem, vmem],
        out_specs=(vmem, vmem, vmem),
        scratch_shapes=[
            pltpu.VMEM((2, BLOCK, cols), f32),
            pltpu.VMEM((ring, BLOCK, cols), bf16),
            pltpu.VMEM((ring, BLOCK, cols), bf16),
            pltpu.VMEM((2 * pairs, cols), bf16),
            pltpu.VMEM((2 * pairs, cols), f32),
            pltpu.VMEM((R, pr, cols), f32),
            pltpu.VMEM((R, pr, cols), f32),
            pltpu.VMEM((ITERS + 1, R, pr, cols + 128), f32),
            pltpu.VMEM((2 * nb, pairs, BLOCK), f32),
            pltpu.VMEM((2 * nb, pairs, BLOCK), f32),
            pltpu.VMEM((2 * nb, C, pairs, BLOCK), f32),
            pltpu.VMEM((ITERS, pairs, 128), f32),
            pltpu.VMEM((ITERS, pairs, 128), f32),
            pltpu.VMEM((C, ITERS, pairs, 128), f32),
            dma((2,)),
            dma((2 * nb,)), dma((2 * nb,)),
            dma((2 * nb, C)), dma((2 * nb, C)),
            dma((R,)), dma((R,)), dma((R,)), dma((R,)),
            dma((C,)), dma((C,)),
        ],
        compiler_params=pltpu.CompilerParams(
            collective_id=0, has_side_effects=True, vmem_limit_bytes=62 << 20),
    )(kernel, source, target.reshape(R, pr, cols))
    return u, v, jnp.sum(e, axis=2) / (cols * D)


def solution(mesh):
    R, C, K = (mesh.shape[a] for a in ("row", "col", "rep"))
    return jax.shard_map(
        functools.partial(local, R, C, C * K),
        mesh=mesh,
        in_specs=(
            P(("groups", "row"), ("col", "rep")),
            P("groups", "row"),
            P("groups", ("col", "rep")),
        ),
        out_specs=(P("groups", "row"), P("groups", ("col", "rep")), P("groups", None)),
        check_vma=False,
    )
```

```python
import functools

import jax
import jax.numpy as jnp
from jax import lax
from jax.experimental import pallas as pl
from jax.experimental.pallas import tpu as pltpu
from jax.sharding import PartitionSpec as P

ITERS = 3
BLOCK = 256
CHUNK = 1024
LAG = 3
KEPT = 6
MESH = pl.DeviceIdType.MESH


def split(x):
    hi = x.astype(jnp.bfloat16)
    return hi, (x - hi.astype(jnp.float32)).astype(jnp.bfloat16)


def body(R, C, k_hbm, src, tgt, u_out, v_out, e_out,
         kf, kh, kl, vhl, acc, red, rsrx, vbuf, part, rx1, rx2, eb, erx1, erx2,
         ksem, s1, r1, s2, r2, srs, rrs, sag, rag, se, re):
    rows, cols = k_hbm.shape
    pairs = src.shape[0]
    nb = rows // BLOCK
    pr = pairs // R
    kept = min(KEPT, nb - 2)
    ring = kh.shape[0] - kept

    def home(b):
        return jnp.where(b < kept, b, kept + lax.rem(b, ring))

    me_r = lax.axis_index("row")
    me_c = lax.axis_index("col")
    me_k = lax.axis_index("rep")
    other = 1 - me_k

    def load(b):
        return pltpu.make_async_copy(
            k_hbm.at[pl.ds(pl.multiple_of(b * BLOCK, BLOCK), BLOCK), :],
            kf.at[lax.rem(b, 2)], ksem.at[lax.rem(b, 2)])

    load(0).start()
    load(1).start()

    barrier = pltpu.get_barrier_semaphore()
    pl.semaphore_signal(barrier, inc=1, device_id={"rep": other}, device_id_type=MESH)
    for k in range(1, C):
        pl.semaphore_signal(barrier, inc=1, device_id={"col": lax.rem(me_c + k, C)}, device_id_type=MESH)
    for k in range(1, R):
        pl.semaphore_signal(barrier, inc=1, device_id={"row": lax.rem(me_r + k, R)}, device_id_type=MESH)
    pl.semaphore_wait(barrier, 1 + (C - 1) + (R - 1))

    vbuf[0, :, :, 0:cols] = jnp.ones((R, pr, cols), jnp.float32)

    def to_rep(src_ref, dst_ref, ssem, rsem):
        return pltpu.make_async_remote_copy(
            src_ref=src_ref, dst_ref=dst_ref, send_sem=ssem, recv_sem=rsem,
            device_id={"rep": other}, device_id_type=MESH)

    def to_col(k, src_ref, dst_ref, ssem, rsem):
        return pltpu.make_async_remote_copy(
            src_ref=src_ref, dst_ref=dst_ref, send_sem=ssem, recv_sem=rsem,
            device_id={"col": lax.rem(me_c + k, C)}, device_id_type=MESH)

    def to_row(k, src_ref, dst_ref, ssem, rsem):
        return pltpu.make_async_remote_copy(
            src_ref=src_ref, dst_ref=dst_ref, send_sem=ssem, recv_sem=rsem,
            device_id={"row": lax.rem(me_r + k, R)}, device_id_type=MESH)

    def first(g):
        return to_rep(part.at[g], rx1.at[g], s1.at[g], r1.at[g])

    for t in range(ITERS):
        base = (t % 2) * nb
        acc[...] = jnp.zeros_like(acc)

        @pl.loop(0, nb + LAG)
        def _(s):
            @pl.when(s < nb)
            def _():
                hold = home(s)
                fresh = (s >= kept) if t > 0 else (s >= 0)
                dims = (((1,), (1,)), ((), ()))

                @pl.when(fresh)
                def _():
                    slot = lax.rem(s, 2)
                    load(s).wait()
                    if t == 0:
                        lanes = jnp.zeros((BLOCK, 128), jnp.float32)
                        for c in range(0, cols, CHUNK):
                            for d in range(c, c + CHUNK, 128):
                                x = kf[slot, :, d:d + 128]
                                hi, lo = split(x)
                                kh[hold, :, d:d + 128] = hi
                                kl[hold, :, d:d + 128] = lo
                                lanes += x
                        hi, lo = split(lanes)
                        one = jnp.ones((pairs, 128), jnp.bfloat16)
                        part[base + s] = (lax.dot_general(one, hi, dims, preferred_element_type=jnp.float32)
                                          + lax.dot_general(one, lo, dims, preferred_element_type=jnp.float32))
                    else:
                        total = jnp.zeros((2 * pairs, BLOCK), jnp.float32)
                        for c in range(0, cols, CHUNK):
                            for d in range(c, c + CHUNK, 128):
                                hi, lo = split(kf[slot, :, d:d + 128])
                                kh[hold, :, d:d + 128] = hi
                                kl[hold, :, d:d + 128] = lo
                            v = vhl[:, c:c + CHUNK]
                            total += lax.dot_general(v, kh[hold, :, c:c + CHUNK], dims,
                                                     preferred_element_type=jnp.float32)
                            total += lax.dot_general(v, kl[hold, :, c:c + CHUNK], dims,
                                                     preferred_element_type=jnp.float32)
                        part[base + s] = total[:pairs] + total[pairs:]

                    @pl.when(s + 2 < nb)
                    def _():
                        load(s + 2).start()
                    if t < ITERS - 1:
                        @pl.when(s + 2 >= nb)
                        def _():
                            load(s + 2 - nb + kept).start()

                if t > 0:
                    @pl.when(s < kept)
                    def _():
                        v = vhl[...]
                        total = (lax.dot_general(v, kh[hold], dims, preferred_element_type=jnp.float32)
                                 + lax.dot_general(v, kl[hold], dims, preferred_element_type=jnp.float32))
                        part[base + s] = total[:pairs] + total[pairs:]

                first(base + s).start()

            @pl.when((s >= 1) & (s <= nb))
            def _():
                g = base + s - 1
                first(g).wait()
                rx2[g, me_c] = part[g] + rx1[g]
                for k in range(1, C):
                    to_col(k, rx2.at[g, me_c], rx2.at[g, me_c], s2.at[g, k], r2.at[g, k]).start()

            @pl.when(s >= LAG)
            def _():
                b = s - LAG
                g = base + b
                hold = home(b)
                for k in range(1, C):
                    peer = lax.rem(me_c + (C - k), C)
                    to_col(k, rx2.at[g, peer], rx2.at[g, peer], s2.at[g, k], r2.at[g, k]).wait()
                kv = rx2[g, 0]
                for c in range(1, C):
                    kv += rx2[g, c]
                at = pl.ds(pl.multiple_of(b * BLOCK, BLOCK), BLOCK)
                u = src[:, at] / kv
                u_out[:, at] = u
                hi, lo = split(u)
                uhl = jnp.concatenate([hi, lo], axis=0)
                acc[...] += (jnp.dot(uhl, kh[hold], preferred_element_type=jnp.float32)
                             + jnp.dot(uhl, kl[hold], preferred_element_type=jnp.float32))

        for q in range(R):
            red[q] = acc[q * pr:(q + 1) * pr, :] + acc[pairs + q * pr:pairs + (q + 1) * pr, :]
        for k in range(1, R):
            to_row(k, red.at[lax.rem(me_r + k, R)], rsrx.at[me_r], srs.at[k], rrs.at[k]).start()
        total = red[me_r]
        for k in range(1, R):
            peer = lax.rem(me_r + (R - k), R)
            to_row(k, red.at[lax.rem(me_r + k, R)], rsrx.at[peer], srs.at[k], rrs.at[k]).wait()
            total += rsrx[peer]
        goal = tgt[me_r]
        diff = jnp.abs(vbuf[t, me_r, :, 0:cols] * total - goal)
        lanes = diff[:, 0:128]
        for c in range(128, cols, 128):
            lanes += diff[:, c:c + 128]
        vbuf[t + 1, me_r, :, 0:cols] = goal / total
        vbuf[t + 1, me_r, :, cols:cols + 128] = lanes
        for k in range(1, R):
            to_row(k, vbuf.at[t + 1, me_r], vbuf.at[t + 1, me_r], sag.at[k], rag.at[k]).start()
        for k in range(1, R):
            peer = lax.rem(me_r + (R - k), R)
            to_row(k, vbuf.at[t + 1, peer], vbuf.at[t + 1, peer], sag.at[k], rag.at[k]).wait()
        full = jnp.concatenate([vbuf[t + 1, q, :, 0:cols] for q in range(R)], axis=0)
        if t < ITERS - 1:
            hi, lo = split(full)
            vhl[0:pairs, :] = hi
            vhl[pairs:, :] = lo
        else:
            v_out[...] = full
        eb[t] = jnp.concatenate([vbuf[t + 1, q, :, cols:cols + 128] for q in range(R)], axis=0)

    swap = to_rep(eb, erx1, se.at[0], re.at[0])
    swap.start()
    swap.wait()
    erx2[me_c] = eb[...] + erx1[...]
    for k in range(1, C):
        to_col(k, erx2.at[me_c], erx2.at[me_c], se.at[k], re.at[k]).start()
    for k in range(1, C):
        peer = lax.rem(me_c + (C - k), C)
        to_col(k, erx2.at[peer], erx2.at[peer], se.at[k], re.at[k]).wait()
    e = erx2[0]
    for c in range(1, C):
        e += erx2[c]
    e_out[...] = e


def local(R, C, D, kernel, source, target):
    rows, cols = kernel.shape
    pairs = source.shape[0]
    pr = pairs // R
    nb = rows // BLOCK
    f32, bf16 = jnp.float32, jnp.bfloat16
    dma = pltpu.SemaphoreType.DMA
    vmem = pl.BlockSpec(memory_space=pltpu.VMEM)
    ring = LAG + 1 + min(KEPT, nb - 2)
    u, v, e = pl.pallas_call(
        functools.partial(body, R, C),
        out_shape=(
            jax.ShapeDtypeStruct((pairs, rows), f32),
            jax.ShapeDtypeStruct((pairs, cols), f32),
            jax.ShapeDtypeStruct((ITERS, pairs, 128), f32),
        ),
        in_specs=[pl.BlockSpec(memory_space=pl.ANY), vmem, vmem],
        out_specs=(vmem, vmem, vmem),
        scratch_shapes=[
            pltpu.VMEM((2, BLOCK, cols), f32),
            pltpu.VMEM((ring, BLOCK, cols), bf16),
            pltpu.VMEM((ring, BLOCK, cols), bf16),
            pltpu.VMEM((2 * pairs, cols), bf16),
            pltpu.VMEM((2 * pairs, cols), f32),
            pltpu.VMEM((R, pr, cols), f32),
            pltpu.VMEM((R, pr, cols), f32),
            pltpu.VMEM((ITERS + 1, R, pr, cols + 128), f32),
            pltpu.VMEM((2 * nb, pairs, BLOCK), f32),
            pltpu.VMEM((2 * nb, pairs, BLOCK), f32),
            pltpu.VMEM((2 * nb, C, pairs, BLOCK), f32),
            pltpu.VMEM((ITERS, pairs, 128), f32),
            pltpu.VMEM((ITERS, pairs, 128), f32),
            pltpu.VMEM((C, ITERS, pairs, 128), f32),
            dma((2,)),
            dma((2 * nb,)), dma((2 * nb,)),
            dma((2 * nb, C)), dma((2 * nb, C)),
            dma((R,)), dma((R,)), dma((R,)), dma((R,)),
            dma((C,)), dma((C,)),
        ],
        compiler_params=pltpu.CompilerParams(
            collective_id=0, has_side_effects=True, vmem_limit_bytes=62 << 20),
    )(kernel, source, target.reshape(R, pr, cols))
    return u, v, jnp.sum(e, axis=2) / (cols * D)


def solution(mesh):
    R, C, K = (mesh.shape[a] for a in ("row", "col", "rep"))
    return jax.shard_map(
        functools.partial(local, R, C, C * K),
        mesh=mesh,
        in_specs=(
            P(("groups", "row"), ("col", "rep")),
            P("groups", "row"),
            P("groups", ("col", "rep")),
        ),
        out_specs=(P("groups", "row"), P("groups", ("col", "rep")), P("groups", None)),
        check_vma=False,
    )
```
